32 devices in a mesh: tm: 8 (over z, x), rows: 4 (over y, core).
Axes of the slice: x: 2, y: 2, z: 4, core: 2. Of those that a mesh axis runs over, the one named last changes fastest.
Arguments:
- observations: float32 [8, 2048], P('tm'), may hold values from -48 to 48
- site_ids: int32 [8, 2048], P('tm'), may hold values from 0 to 4095
- counts: int32 [8], P('tm'), may hold values from 1 to 2048, 12288 in all
- frequencies: float32 [128], replicated, may hold values from -3.140625 to 3.140625
- decay: float32 [128], replicated, may hold values from 0.02 to 0.2
- proc_var: float32 [128], replicated, may hold values from 0.05 to 0.2
Outputs:
- smooth_mean: float32 [8, 256], P('tm', 'rows')
- smooth_cov: float32 [8, 256, 256], P('tm', 'rows')
The draws below stay inside these ranges and needn't reach their ends.
Inputs may be any that keep to these rules, and one draw needn't show every extreme that they name: Step t observes the sites in its first counts[t] slots; the other slots are ignored.
All inputs are finite; a program needn't handle non-finite values. No bound on the sum of `counts` on one device may be relied on, other than what follows from the above.
Results may differ from the reference program's by a relative error of at most 0.0003.
Values sent between devices are 32-bit elements; how exact they have to be, the bound alone decides.
A program may use at most 128 MiB of HBM per device.

```python
import math
import jax
import jax.numpy as jnp
import numpy as np
from jax import lax

MODES = 128
SITES = 2048
GRID = 4096
OBS_VAR = 64
STEPS = 8


def with_ends(result, stream_key, low, top_value):
    longest = result.shape.index(max(result.shape))
    spots = []
    for shift in (0, 1):
        where = [jax.random.randint(jax.random.fold_in(stream_key, axis), (), 0, length) for axis, length in enumerate(result.shape)]
        where[longest] = (where[longest] + shift) % result.shape[longest]
        spots.append(tuple(where))
    return result.at[spots[0]].set(low).at[spots[1]].set(top_value)


def steps_of(rng, dims, shards, smallest, high):
    def one(axis_at, blocks):
        heights = jax.random.uniform(jax.random.fold_in(jax.random.fold_in(rng, 6), axis_at), (blocks,), jnp.float32, smallest / len(shards), high / len(shards))
        return jnp.repeat(jnp.exp(heights), dims[axis_at] // blocks).reshape((-1,) + (1,) * (len(dims) - axis_at - 1))

    loudness = one(*shards[0])
    for cut in shards[1:]:
        loudness = loudness * one(*cut)
    return loudness


def profile(amount, total, bound, lean):
    loads = [(1 << 20) // math.isqrt(rank ** lean) + 1 for rank in range(2, amount + 1)]
    rest, given = total - bound - (amount - 1), [1] * (amount - 1)
    while rest > 0:
        candidates = [i for i in range(amount - 1) if given[i] < bound]
        pool, remaining = sum([loads[i] for i in candidates]), rest
        for i in candidates:
            addition = min(bound - given[i], max(1, remaining * loads[i] // pool), rest)
            given[i] = given[i] + addition
            rest = rest - addition
    return np.array([bound] + given)


def ragged_sizes(key, amount, total, most, lean):
    if amount == 2:
        one = jax.random.randint(key, (), max(1, total - most), min(most, total - 1) + 1)
        return jnp.stack([one, total - one])
    sizes = jnp.asarray(profile(amount, total, most, lean), jnp.int32)
    twos = (amount - 1) // 2
    donor, sink = sizes[1:1 + 2 * twos:2], sizes[2:2 + 2 * twos:2]
    room = jnp.minimum(donor - 1, most - sink)
    passed = jax.random.randint(jax.random.fold_in(key, 1), (twos,), 0, 1 << 20) % (room + 1)
    sizes = sizes.at[1:1 + 2 * twos:2].set(donor - passed).at[2:2 + 2 * twos:2].set(sink + passed)
    return sizes[jax.random.permutation(jax.random.fold_in(key, 2), amount)]


def gaussian(stream_key, shape, deviation, bound, split=(), held_as=jnp.bfloat16):
    values = deviation * jax.random.normal(stream_key, shape, jnp.float32)
    if split:
        values = values * steps_of(stream_key, shape, split, -0.22, 0.18)
    return jnp.clip(values, -bound, bound).astype(held_as)


def setup_inputs(seed: int = 0) -> dict:
    key_of = jax.random.split(jax.random.key(seed), 7)
    return {
        "observations": gaussian(key_of[0], (STEPS, SITES), 8.0, 48.0, ((0, 8),), jnp.float32),
        "site_ids": with_ends(jax.random.randint(key_of[1], (STEPS, SITES), 0, GRID), jax.random.fold_in(key_of[1], 1), 0, GRID - 1).astype(jnp.int32),
        "counts": ragged_sizes(key_of[2], STEPS, STEPS * SITES * 3 // 4, SITES, 0).astype(jnp.int32),
        "frequencies": jnp.clip(jax.random.uniform(key_of[3], (MODES,), jnp.float32, -3.140625, 3.140625), -3.140625, 3.140625),
        "decay": jnp.clip(jnp.exp(jax.random.uniform(key_of[4], (MODES,), jnp.float32, math.log(0.02), math.log(0.2))), 0.02, 0.2),
        "proc_var": jnp.clip(jnp.exp(jax.random.uniform(key_of[5], (MODES,), jnp.float32, math.log(0.05), math.log(0.2))), 0.05, 0.2),
    }


exact_mode = lax.Precision.HIGHEST

def product(left, right):
    return jnp.dot(left.astype(jnp.float32), right.astype(jnp.float32), precision=exact_mode, preferred_element_type=jnp.float32)

def rotate_rows(matrix, damping, cosines, sines, backward):
    width = matrix.shape[0]
    pairs = matrix.reshape((width // 2, 2) + matrix.shape[1:])
    expand = (width // 2,) + (1,) * (matrix.ndim - 1)
    damp_part = damping.reshape(expand)
    cos_part = cosines.reshape(expand)
    sin_part = sines.reshape(expand)
    upper = pairs[:, 0]
    lower = pairs[:, 1]
    if backward:
        new_upper = damp_part * (cos_part * upper + sin_part * lower)
        new_lower = damp_part * (cos_part * lower - sin_part * upper)
    else:
        new_upper = damp_part * (cos_part * upper - sin_part * lower)
        new_lower = damp_part * (sin_part * upper + cos_part * lower)
    return jnp.stack([new_upper, new_lower], axis=1).reshape(matrix.shape)

def rotate_cols(matrix, damping, cosines, sines, transposed):
    return rotate_rows(matrix.T, damping, cosines, sines, not transposed).T

def site_features(site_row, live, modes):
    slots = jnp.arange(site_row.shape[0], dtype=jnp.int32)
    weights = (slots < live).astype(jnp.float32)
    orders = jnp.arange(1, modes + 1, dtype=jnp.int32)
    phase = site_row[:, None] * orders[None, :] % GRID
    angles = phase.astype(jnp.float32) * (2.0 * math.pi / GRID)
    features = jnp.stack([jnp.cos(angles), jnp.sin(angles)], axis=-1)
    features = features.reshape(site_row.shape[0], 2 * modes) * (1.0 / math.sqrt(modes))
    return (features, weights)

def gram(weighted, features):
    return lax.dot_general(weighted.astype(jnp.float32), features.astype(jnp.float32), (((0,), (0,)), ((), ())), precision=exact_mode, preferred_element_type=jnp.float32)

def build_element(precision_obs, info_obs, first, damping, cosines, sines, proc_var):
    per_mode = jnp.where(first, (1.0 - damping * damping) / proc_var, 1.0 / proc_var)
    diag_prec = jnp.repeat(per_mode, 2)
    keep = jnp.where(first, 0.0, 1.0).astype(jnp.float32)
    width = diag_prec.shape[0]
    factor = jnp.linalg.cholesky(jnp.diag(diag_prec) + precision_obs)
    covariance = jax.scipy.linalg.cho_solve((factor, True), jnp.eye(width, dtype=jnp.float32))
    shift_vec = product(covariance, info_obs)
    trans = rotate_cols(covariance * diag_prec[None, :], damping, cosines, sines, False) * keep
    inner_mat = jnp.diag(diag_prec) - diag_prec[:, None] * covariance * diag_prec[None, :]
    prec_mat = rotate_cols(rotate_rows(inner_mat, damping, cosines, sines, True), damping, cosines, sines, False) * keep
    info_vec = rotate_rows(diag_prec * shift_vec, damping, cosines, sines, True) * keep
    return (trans, shift_vec, covariance, info_vec, prec_mat)

def combine(earlier, later):
    a_trans, a_shift, a_cov, a_info, a_prec = earlier
    b_trans, b_shift, b_cov, b_info, b_prec = later
    width = a_cov.shape[0]
    factor = jnp.linalg.cholesky(a_cov)
    inner_mat = jnp.eye(width, dtype=jnp.float32) + product(product(factor.T, b_prec), factor)
    inner_fac = jnp.linalg.cholesky(inner_mat)
    solved = jax.scipy.linalg.cho_solve((inner_fac, True), product(factor.T, b_trans.T)).T
    gain_cov = product(solved, factor.T)
    gain_dyn = b_trans - product(gain_cov, b_prec)
    new_trans = product(gain_dyn, a_trans)
    new_shift = product(gain_dyn, a_shift) + product(gain_cov, b_info) + b_shift
    new_cov = product(gain_cov, b_trans.T) + b_cov
    back_prec = product(a_trans.T, b_prec)
    weight_solve = jax.scipy.linalg.cho_solve((inner_fac, True), product(factor.T, back_prec.T)).T
    weight_cov = product(weight_solve, factor.T)
    back_map = a_trans.T - weight_cov
    back_full = back_prec - product(weight_cov, b_prec)
    new_info = product(back_map, b_info) - product(back_full, a_shift) + a_info
    new_prec = product(back_full, a_trans) + a_prec
    return (new_trans, new_shift, new_cov, new_info, new_prec)

def smooth_element(mean, covariance, last, damping, cosines, sines, proc_var):
    keep = jnp.where(last, 0.0, 1.0).astype(jnp.float32)
    forward_cov = rotate_rows(covariance, damping, cosines, sines, False)
    predicted = rotate_cols(forward_cov, damping, cosines, sines, True) + jnp.diag(jnp.repeat(proc_var, 2))
    gain = jax.scipy.linalg.cho_solve((jnp.linalg.cholesky(predicted), True), forward_cov).T
    moved_mean = rotate_rows(mean, damping, cosines, sines, False)
    smooth_shift = mean - keep * product(gain, moved_mean)
    smooth_rest = covariance - keep * product(gain, forward_cov)
    return (gain * keep, smooth_shift, smooth_rest)

def smooth_combine(earlier, later):
    a_gain, a_shift, a_rest = earlier
    b_gain, b_shift, b_rest = later
    return (product(a_gain, b_gain), product(a_gain, b_shift) + a_shift, product(product(a_gain, b_rest), a_gain.T) + a_rest)

def reference(observations, site_ids, counts, frequencies, decay, proc_var):
    damping = jnp.exp(-decay)
    cosines = jnp.cos(frequencies)
    sines = jnp.sin(frequencies)
    modes = frequencies.shape[0]
    total = observations.shape[0]
    indices = jnp.arange(total, dtype=jnp.int32)
    noise_scale = 1.0 / OBS_VAR

    def element_at(packed):
        site_row, obs_row, live, index = packed
        features, weights = site_features(site_row, live, modes)
        weighted = features * weights[:, None]
        precision_obs = gram(weighted, features) * noise_scale
        info_obs = jnp.dot((obs_row * weights).astype(jnp.float32), features.astype(jnp.float32), precision=exact_mode, preferred_element_type=jnp.float32) * noise_scale
        return build_element(precision_obs, info_obs, index == 0, damping, cosines, sines, proc_var)
    elements = lax.map(element_at, (site_ids, observations, counts, indices))
    head = jax.tree.map(lambda whole: whole[0], elements)
    others = jax.tree.map(lambda whole: whole[1:], elements)

    def forward(carry, element):
        merged = combine(carry, element)
        return (merged, (merged[1], merged[2]))
    _, (means_rest, covs_rest) = lax.scan(forward, head, others)
    means = jnp.concatenate([head[1][None], means_rest], axis=0)
    covs = jnp.concatenate([head[2][None], covs_rest], axis=0)

    def smooth_at(packed):
        mean, covariance, index = packed
        return smooth_element(mean, covariance, index == total - 1, damping, cosines, sines, proc_var)
    smoothing = lax.map(smooth_at, (means, covs, indices))
    tail = jax.tree.map(lambda whole: whole[-1], smoothing)
    before = jax.tree.map(lambda whole: whole[:-1], smoothing)

    def backward(carry, element):
        merged = smooth_combine(element, carry)
        return (merged, (merged[1], merged[2]))
    _, (shift_rest, rest_rest) = lax.scan(backward, tail, before, reverse=True)
    smooth_mean = jnp.concatenate([shift_rest, tail[1][None]], axis=0)
    smooth_cov = jnp.concatenate([rest_rest, tail[2][None]], axis=0)
    return (smooth_mean, smooth_cov)
```

```python
import functools
import math

import jax
import jax.numpy as jnp
from jax import lax
from jax.experimental import pallas as pl
from jax.experimental.pallas import tpu as pltpu
from jax.sharding import PartitionSpec as P

GRID = 4096
OBS_VAR = 64
TOLERANCE = 3e-5
FINE = 16

exact_mode = lax.Precision.HIGHEST


def exact(left, right):
    return jnp.dot(left, right, precision=exact_mode, preferred_element_type=jnp.float32)


def coarse(left, right):
    return jnp.dot(
        left.astype(jnp.bfloat16), right.astype(jnp.bfloat16), preferred_element_type=jnp.float32
    )


def halves(value):
    high = value.astype(jnp.bfloat16)
    return high, (value - high.astype(jnp.float32)).astype(jnp.bfloat16)


def product(left, right):
    left_high, left_low = left if isinstance(left, tuple) else halves(left)
    right_high, right_low = right if isinstance(right, tuple) else halves(right)
    dot = functools.partial(jnp.dot, preferred_element_type=jnp.float32)
    return dot(left_high, right_high) + (dot(left_high, right_low) + dot(left_low, right_high))


def site_sums(site_row, obs_row, live, modes):
    count = site_row.shape[0]
    weights = (jnp.arange(count, dtype=jnp.int32) < live).astype(jnp.float32)
    groups = 2 * modes // FINE
    steps = jnp.arange(groups, dtype=jnp.int32) * FINE
    exponents = jnp.concatenate(
        [steps - modes, 2 * modes + 1 - steps, steps[: groups // 2] + 1, jnp.arange(FINE)]
    ).astype(jnp.int32)
    phase = (exponents[:, None] * site_row[None, :]) % GRID
    angles = phase.astype(jnp.float32) * (2.0 * math.pi / GRID)
    cosines, sines = jnp.cos(angles), jnp.sin(angles)
    last = exponents.shape[0] - FINE
    scale = jnp.where(jnp.arange(last)[:, None] < 2 * groups, weights[None, :], (weights * obs_row)[None, :])
    left = jnp.concatenate([cosines[:last] * scale, sines[:last] * scale], axis=0)
    right = jnp.concatenate([cosines[last:], sines[last:]], axis=0)
    sums = lax.dot_general(
        left, right, (((1,), (1,)), ((), ())), precision=exact_mode, preferred_element_type=jnp.float32
    )
    cc, cs = sums[:last, :FINE], sums[:last, FINE:]
    sc, ss = sums[last:, :FINE], sums[last:, FINE:]
    one, two = groups, 2 * groups
    near_cos = (cc - ss)[:one].reshape(-1)
    near_sin = (sc + cs)[:one].reshape(-1)
    far_cos = (cc + ss)[one:two].reshape(-1)
    far_sin = (sc - cs)[one:two].reshape(-1)
    info = jnp.concatenate([(cc - ss)[two:].reshape(-1), (sc + cs)[two:].reshape(-1)])
    empty = jnp.zeros_like(info)
    return jnp.stack([near_cos, near_sin, far_cos, far_sin, info, empty, empty, empty])


def invert(sources, splits, targets, low, high):
    width = sources[0].shape[-1]
    rows = lax.broadcasted_iota(jnp.int32, (width, width), 0)
    unit = jnp.where(rows == lax.broadcasted_iota(jnp.int32, (width, width), 1), 1.0, 0.0)
    center = (high + low) / (high - low)
    slope = 2.0 / (high - low)
    top = 2.0 * center * center - 1.0
    for source, split, target in zip(sources, splits, targets):
        matrix = source[...]
        split[0], split[1] = halves(matrix)
        target[...] = (4.0 * center * slope / top) * unit - (2.0 * slope * slope / top) * matrix

    def body(radius):
        factor = 2.0 / (2.0 - radius * radius)
        residues = [
            unit - product((split[0], split[1]), target[...])
            for split, target in zip(splits, targets)
        ]
        for target, residue in zip(targets, residues):
            target[...] = factor * (target[...] + coarse(target[...], residue))
        return radius * radius / (2.0 - radius * radius)

    lax.while_loop(lambda radius: radius > TOLERANCE, body, 1.0 / top)


def solve_kernel(
    where_ref, bounds_ref, sums_ref, turn_ref, turn_cols_ref, damp_ref, damp_cols_ref,
    mean_ref, cov_ref, diag, link, back, info, split, inverse,
):
    steps = sums_ref.shape[0]
    width = sums_ref.shape[2]
    modes = width // 2
    own = where_ref[0]
    block_row = where_ref[1]
    rows = lax.broadcasted_iota(jnp.int32, (width, width), 0)
    cols = lax.broadcasted_iota(jnp.int32, (width, width), 1)
    unit = jnp.where(rows == cols, 1.0, 0.0)
    small_rows = lax.broadcasted_iota(jnp.int32, (modes, modes), 0)
    small_cols = lax.broadcasted_iota(jnp.int32, (modes, modes), 1)
    mirror = jnp.where(small_rows + small_cols == modes - 1, 1.0, 0.0)
    scale = 0.5 / (OBS_VAR * modes)
    info_scale = 1.0 / (OBS_VAR * math.sqrt(modes))
    damp = damp_ref[0:1, :]
    damp_col = damp_cols_ref[:, 0:1]
    wide = damp * damp
    damp_sq = jnp.concatenate([wide, wide], axis=1)

    def shifted(row):
        spread = jnp.broadcast_to(row, (modes, width))
        return pltpu.roll(spread, modes, 1, stride=1, stride_axis=0)[:, :modes]

    most = jnp.zeros((1, width), jnp.float32)
    for step in range(steps):
        near_cos = shifted(sums_ref[step, 0:1, :])
        near_sin = shifted(sums_ref[step, 1:2, :])
        far = jnp.concatenate(
            [shifted(sums_ref[step, 2:3, :]), shifted(sums_ref[step, 3:4, :])], axis=0
        )
        far = exact(far, mirror)
        far_cos, far_sin = far[:modes], far[modes:]
        cosines = turn_ref[step, 0:1, :] * scale
        sines = turn_ref[step, 1:2, :] * scale
        cos_col = turn_cols_ref[step, :, 0:1]
        sin_col = turn_cols_ref[step, :, 1:2]
        up_a, up_b = near_cos + far_cos, far_sin + near_sin
        low_a, low_b = far_sin - near_sin, near_cos - far_cos
        up_left, up_right = up_a * cosines + up_b * sines, up_b * cosines - up_a * sines
        low_left, low_right = low_a * cosines + low_b * sines, low_b * cosines - low_a * sines
        top = jnp.concatenate(
            [cos_col * up_left + sin_col * low_left, cos_col * up_right + sin_col * low_right], axis=1
        )
        bottom = jnp.concatenate(
            [cos_col * low_left - sin_col * up_left, cos_col * low_right - sin_col * up_right], axis=1
        )
        whole = jnp.concatenate([top, bottom], axis=0)
        most = jnp.maximum(most, jnp.sum(jnp.abs(whole), axis=0, keepdims=True))
        edge = 1.0 if step in (0, steps - 1) else 1.0 + damp_sq
        diag[step] = whole + unit * edge
        info_cos, info_sin = sums_ref[step, 4:5, :modes], sums_ref[step, 4:5, modes:]
        turn_cos, turn_sin = turn_ref[step, 0:1, :] * info_scale, turn_ref[step, 1:2, :] * info_scale
        turned = jnp.concatenate(
            [turn_cos * info_cos + turn_sin * info_sin, turn_cos * info_sin - turn_sin * info_cos], axis=1
        )
        info[step] = jnp.broadcast_to(turned, (8, width))
    high = jnp.max(most) + bounds_ref[0]

    def place(position, amount, flipped):
        return jnp.where(flipped, amount - 1 - position, position)

    damp_wide = jnp.concatenate([damp, damp], axis=1)
    damp_tall = jnp.concatenate([damp_col, damp_col], axis=0)
    amount, index, level = steps, own, 0
    base, link_base = 0, 0
    diag_at, link_at = 0, 0
    while amount > 1:
        half = amount // 2
        flipped = lax.rem(index, 2) == 1
        links = amount - 1
        out_base = diag_at + amount
        chunk = min(4, half)
        for start in range(0, half, chunk):
            picks = [diag_at + place(2 * k + 1, amount, flipped) for k in range(start, start + chunk)]
            invert(
                [diag.at[pick] for pick in picks],
                [split.at[k] for k in range(chunk)],
                [inverse.at[k] for k in range(start, start + chunk)],
                bounds_ref[1 + level],
                high,
            )
        for k in range(half):
            kept = diag_at + place(2 * k, amount, flipped)
            diag[out_base + k] = diag[kept]
            info[out_base + k] = info[kept]
        out_links = link_at + (links if level else 0)
        for k in range(half):
            gone = info[diag_at + place(2 * k + 1, amount, flipped)]
            matrix = inverse[k]
            if level == 0:
                moved = damp_tall * matrix * damp_wide
                passed = product(gone * 1.0, matrix) * damp_wide
                diag[out_base + k] -= moved
                info[out_base + k] += passed
                if k + 1 < half:
                    diag[out_base + k + 1] -= moved
                    info[out_base + k + 1] += passed
                    link[out_links + k] = moved
                    back[out_links + k] = moved
                continue
            here = link_at + place(2 * k, links, flipped)
            forth, revert = link[here], back[here]
            forth, revert = jnp.where(flipped, revert, forth), jnp.where(flipped, forth, revert)
            forth, revert, matrix = halves(forth), halves(revert), halves(matrix)
            left = halves(product(matrix, revert))
            diag[out_base + k] -= product(forth, left)
            info[out_base + k] += product(gone, left)
            if k + 1 < half:
                after = link_at + place(2 * k + 1, links, flipped)
                next_forth, next_revert = link[after], back[after]
                next_forth, next_revert = (
                    halves(jnp.where(flipped, next_revert, next_forth)),
                    halves(jnp.where(flipped, next_forth, next_revert)),
                )
                right = halves(product(matrix, next_forth))
                diag[out_base + k + 1] -= product(next_revert, right)
                info[out_base + k + 1] += product(gone, right)
                link[out_links + k] = product(forth, right)
                back[out_links + k] = product(next_revert, left)
        index = place(index, amount, flipped) // 2
        diag_at, link_at = out_base, out_links
        amount, level = half, level + 1

    invert([diag.at[diag_at]], [split.at[0]], [inverse.at[0]], bounds_ref[1 + level], high)
    result = inverse[0]
    state = exact(info[diag_at], result)[0:1]
    cosines, sines = turn_ref[own, 0:1, :], turn_ref[own, 1:2, :]
    cos_col, sin_col = turn_cols_ref[own, :, 0:1], turn_cols_ref[own, :, 1:2]
    left, right = result[:, :modes], result[:, modes:]
    left, right = left * cosines - right * sines, left * sines + right * cosines
    result = jnp.concatenate([left, right], axis=1)
    upper, lower = result[:modes], result[modes:]
    result = jnp.concatenate(
        [cos_col * upper - sin_col * lower, sin_col * upper + cos_col * lower], axis=0
    )
    first, second = state[:, :modes], state[:, modes:]
    state = jnp.concatenate([first * cosines - second * sines, first * sines + second * cosines], axis=1)
    block = cov_ref.shape[0]
    out_rows = lax.broadcasted_iota(jnp.int32, (block, width), 0) + block_row * block
    out_cols = lax.broadcasted_iota(jnp.int32, (block, width), 1)
    pick = jnp.where(out_cols == out_rows // 2 + lax.rem(out_rows, 2) * modes, 1.0, 0.0)
    spread = jnp.where(rows == cols // 2 + lax.rem(cols, 2) * modes, 1.0, 0.0)
    cov_ref[...] = exact(exact(pick, result), spread)
    mean_ref[...] = exact(jnp.broadcast_to(state, (8, width)), spread)


def local(observations, site_ids, counts, frequencies, decay, proc_var):
    modes = frequencies.shape[0]
    width = 2 * modes
    steps = lax.axis_size("tm") * observations.shape[0]
    own = lax.axis_index("tm")
    row_index = lax.axis_index("rows")
    block = width // lax.axis_size("rows")
    sums = site_sums(site_ids[0], observations[0], counts[0], modes)
    sums = lax.all_gather(sums, "tm")
    damping = jnp.exp(-decay)
    root = jnp.sqrt(proc_var)
    times = jnp.arange(steps, dtype=jnp.float32)[:, None]
    turn = jnp.stack([root * jnp.cos(times * frequencies), root * jnp.sin(times * frequencies)], axis=1)
    squared = damping * damping
    levels = (steps - 1).bit_length()
    rest = 1.0 - squared
    bounds = [1.0 + jnp.max(squared)]
    bounds += [jnp.min(rest / (1.0 - jnp.exp(decay * (-2.0 * (1 << level))))) for level in range(levels)]
    bounds += [jnp.min(rest)]
    bounds = jnp.stack(bounds) * jnp.array([1.001] + [0.999] * (levels + 1), jnp.float32)
    damp = jnp.broadcast_to(damping[None, :], (8, modes))
    vmem = pl.BlockSpec(memory_space=pltpu.VMEM)
    smem = pl.BlockSpec(memory_space=pltpu.SMEM)
    mean, cov = pl.pallas_call(
        solve_kernel,
        out_shape=(
            jax.ShapeDtypeStruct((8, width), jnp.float32),
            jax.ShapeDtypeStruct((block, width), jnp.float32),
        ),
        in_specs=[smem, smem, vmem, vmem, vmem, vmem, vmem],
        out_specs=(vmem, vmem),
        scratch_shapes=[
            pltpu.VMEM((2 * steps, width, width), jnp.float32),
            pltpu.VMEM((steps, width, width), jnp.float32),
            pltpu.VMEM((steps, width, width), jnp.float32),
            pltpu.VMEM((2 * steps, 8, width), jnp.float32),
            pltpu.VMEM((4, 2, width, width), jnp.bfloat16),
            pltpu.VMEM((max(1, steps // 2), width, width), jnp.float32),
        ],
        name="solve",
    )(
        jnp.stack([own, row_index]).astype(jnp.int32),
        bounds,
        sums,
        turn,
        jnp.swapaxes(turn, 1, 2),
        damp,
        damp.T,
    )
    mean = lax.dynamic_slice_in_dim(mean[0], row_index * block, block, 0)
    return (mean[None], cov[None])


def solution(mesh):
    return jax.shard_map(
        local,
        mesh=mesh,
        in_specs=(P("tm", None), P("tm", None), P("tm"), P(), P(), P()),
        out_specs=(P("tm", "rows"), P("tm", "rows", None)),
        check_vma=False,
    )
```

```python
import functools
import math

import jax
import jax.numpy as jnp
from jax import lax
from jax.experimental import pallas as pl
from jax.experimental.pallas import tpu as pltpu
from jax.sharding import PartitionSpec as P

GRID = 4096
OBS_VAR = 64
TOLERANCE = 3e-5
FINE = 16

exact_mode = lax.Precision.HIGHEST


def exact(left, right):
    return jnp.dot(left, right, precision=exact_mode, preferred_element_type=jnp.float32)


def coarse(left, right):
    return jnp.dot(
        left.astype(jnp.bfloat16), right.astype(jnp.bfloat16), preferred_element_type=jnp.float32
    )


def halves(value):
    high = value.astype(jnp.bfloat16)
    return high, (value - high.astype(jnp.float32)).astype(jnp.bfloat16)


def product(left, right):
    left_high, left_low = left if isinstance(left, tuple) else halves(left)
    right_high, right_low = right if isinstance(right, tuple) else halves(right)
    dot = functools.partial(jnp.dot, preferred_element_type=jnp.float32)
    return dot(left_high, right_high) + (dot(left_high, right_low) + dot(left_low, right_high))


def parts(value, unit):
    marked = value * unit
    off = value - marked
    column = jnp.sum(marked, axis=1, keepdims=True)
    row = jnp.sum(marked, axis=0, keepdims=True)
    return value, off, halves(off), column, row


def near(left, right):
    return product(left[2], right[2]) + left[3] * right[0] + left[1] * right[4]


def along(row, right):
    return product(row, right[2]) + row * right[4]


def circle(angle):
    square = angle * angle
    cosine = 1.0 / 40320.0 - square * (1.0 / 3628800.0)
    cosine = 1.0 - square * (0.5 - square * (1.0 / 24.0 - square * (1.0 / 720.0 - square * cosine)))
    sine = 1.0 / 5040.0 - square * (1.0 / 362880.0)
    sine = angle * (1.0 - square * (1.0 / 6.0 - square * (1.0 / 120.0 - square * sine)))
    return cosine, sine


def quarter_turn(quadrant, cosine, sine):
    odd = (quadrant & 1) == 1
    new_cosine = jnp.where(odd, sine, cosine)
    new_sine = jnp.where(odd, cosine, sine)
    new_cosine = jnp.where(((quadrant + 1) & 2) == 2, -new_cosine, new_cosine)
    new_sine = jnp.where((quadrant & 2) == 2, -new_sine, new_sine)
    return new_cosine, new_sine


def share_kernel(
    tm_axis, counts_ref, site_ref, obs_ref, freq_ref, decay_ref, var_ref,
    sums_ref, turn_ref, cols_ref, damp_ref, damp_cols_ref, mine, held, send_sem, recv_sem,
):
    count = lax.axis_size(tm_axis)
    own = lax.axis_index(tm_axis)
    sites = site_ref.shape[1]
    modes = freq_ref.shape[1]
    steps = sums_ref.shape[0]
    barrier = pltpu.get_barrier_semaphore()
    for offset in range(1, count):
        pl.semaphore_signal(
            barrier, inc=1, device_id={tm_axis: lax.rem(own + offset, count)},
            device_id_type=pl.DeviceIdType.MESH,
        )

    groups = 2 * modes // FINE
    total = 2 * groups + groups // 2 + FINE
    last = total - FINE
    spot = lax.broadcasted_iota(jnp.int32, (total, sites), 0)
    exponent = jnp.where(spot < groups, spot * FINE - modes, 2 * modes + 1 - (spot - groups) * FINE)
    exponent = jnp.where(spot >= 2 * groups, (spot - 2 * groups) * FINE + 1, exponent)
    exponent = jnp.where(spot >= last, spot - last, exponent)
    phase = (exponent * site_ref[...]) & (GRID - 1)
    quadrant = (phase + GRID // 8) >> int(math.log2(GRID // 4))
    angle = (phase - quadrant * (GRID // 4)).astype(jnp.float32) * (2.0 * math.pi / GRID)
    cosines, sines = quarter_turn(quadrant, *circle(angle))
    slots = lax.broadcasted_iota(jnp.int32, (1, sites), 1)
    weights = jnp.where(slots < counts_ref[0], 1.0, 0.0)
    scale = jnp.where(spot[:last] < 2 * groups, weights, weights * obs_ref[...])
    left = jnp.concatenate([cosines[:last] * scale, sines[:last] * scale], axis=0)
    right = jnp.concatenate([cosines[last:], sines[last:]], axis=0)
    sums = lax.dot_general(
        left, right, (((1,), (1,)), ((), ())), precision=exact_mode, preferred_element_type=jnp.float32
    )
    wide = lax.broadcasted_iota(jnp.int32, (2 * FINE, 2 * modes), 1)
    tall = lax.broadcasted_iota(jnp.int32, (2 * FINE, 2 * modes), 0)
    by_cos = exact(sums, jnp.where(tall == (wide & (FINE - 1)), 1.0, 0.0))
    by_sin = exact(sums, jnp.where(tall - FINE == (wide & (FINE - 1)), 1.0, 0.0))
    one, two = groups, 2 * groups
    cc, cs, sc, ss = by_cos[:last], by_sin[:last], by_cos[last:], by_sin[last:]
    lane = lax.broadcasted_iota(jnp.int32, (groups, 2 * modes), 1)
    keep = jnp.where(lane // FINE == lax.broadcasted_iota(jnp.int32, (groups, 2 * modes), 0), 1.0, 0.0)

    def flat(value):
        return jnp.sum(value * keep[: value.shape[0]], axis=0, keepdims=True)

    near_cos = flat((cc - ss)[:one])
    near_sin = flat((sc + cs)[:one])
    far_cos = flat((cc + ss)[one:two])
    far_sin = flat((sc - cs)[one:two])
    info = jnp.concatenate([flat((cc - ss)[two:])[:, :modes], flat((sc + cs)[two:])[:, :modes]], axis=1)
    empty = jnp.zeros((3, 2 * modes), jnp.float32)
    mine[...] = jnp.concatenate([near_cos, near_sin, far_cos, far_sin, info, empty], axis=0)

    pl.semaphore_wait(barrier, count - 1)
    copies = []
    for offset in range(1, count):
        copy = pltpu.make_async_remote_copy(
            src_ref=mine,
            dst_ref=held.at[offset],
            send_sem=send_sem.at[offset],
            recv_sem=recv_sem.at[offset],
            device_id={tm_axis: lax.rem(own + offset, count)},
            device_id_type=pl.DeviceIdType.MESH,
        )
        copy.start()
        copies.append(copy)

    frequency = freq_ref[...]
    turns = jnp.where(jnp.abs(frequency) > 0.25 * math.pi, 1, 0) + jnp.where(
        jnp.abs(frequency) > 0.75 * math.pi, 1, 0
    )
    turns = jnp.where(frequency < 0.0, -turns, turns)
    share = turns.astype(jnp.float32)
    reduced = (frequency - share * 1.5703125) - share * (0.5 * math.pi - 1.5703125)
    cosine, sine = quarter_turn(turns + 4, *circle(reduced))
    damping = jnp.exp(-decay_ref[...])
    now_cos = jnp.sqrt(var_ref[...])
    now_sin = jnp.zeros_like(now_cos)
    for step in range(steps):
        block = jnp.concatenate([now_cos, now_sin, jnp.zeros((modes - 2, modes), jnp.float32)], axis=0)
        turn_ref[step] = block[:8]
        cols_ref[step] = block.T[:, :8]
        now_cos, now_sin = now_cos * cosine - now_sin * sine, now_cos * sine + now_sin * cosine
    spread = jnp.broadcast_to(damping, (modes, modes))
    damp_ref[...] = spread[:8]
    damp_cols_ref[...] = spread.T[:, :8]

    sums_ref[own] = mine[...]
    for offset in range(1, count):
        copies[offset - 1].wait()
        sums_ref[lax.rem(own + count - offset, count)] = held[offset]


def invert(sources, splits, targets, low, high):
    width = sources[0].shape[-1]
    rows = lax.broadcasted_iota(jnp.int32, (width, width), 0)
    unit = jnp.where(rows == lax.broadcasted_iota(jnp.int32, (width, width), 1), 1.0, 0.0)
    center = (high + low) / (high - low)
    slope = 2.0 / (high - low)
    top = 2.0 * center * center - 1.0
    columns = []
    for source, split, target in zip(sources, splits, targets):
        matrix = source[...]
        columns.append(jnp.sum(matrix * unit, axis=1, keepdims=True))
        split[0], split[1] = halves(matrix * (1.0 - unit))
        target[...] = (4.0 * center * slope / top) * unit - (2.0 * slope * slope / top) * matrix

    def body(radius):
        factor = 2.0 / (2.0 - radius * radius)
        residues = []
        for source, split, target, column in zip(sources, splits, targets, columns):
            marked = target[...] * unit
            row = jnp.sum(marked, axis=0, keepdims=True)
            residues.append(
                (unit - column * target[...])
                - (source[...] * (1.0 - unit)) * row
                - product((split[0], split[1]), target[...] - marked)
            )
        for target, residue in zip(targets, residues):
            target[...] = factor * (target[...] + coarse(target[...], residue))
        return radius * radius / (2.0 - radius * radius)

    lax.while_loop(lambda radius: radius > TOLERANCE, body, 1.0 / top)


def solve_kernel(
    tm_axis, rows_axis, sums_ref, turn_ref, turn_cols_ref, damp_ref, damp_cols_ref,
    mean_ref, cov_ref, diag, link, back, info, split, inverse,
):
    steps = sums_ref.shape[0]
    width = sums_ref.shape[2]
    modes = width // 2
    own = lax.axis_index(tm_axis)
    block_row = lax.axis_index(rows_axis)
    rows = lax.broadcasted_iota(jnp.int32, (width, width), 0)
    cols = lax.broadcasted_iota(jnp.int32, (width, width), 1)
    unit = jnp.where(rows == cols, 1.0, 0.0)
    small_rows = lax.broadcasted_iota(jnp.int32, (modes, modes), 0)
    small_cols = lax.broadcasted_iota(jnp.int32, (modes, modes), 1)
    mirror = jnp.where(small_rows + small_cols == modes - 1, 1.0, 0.0)
    scale = 0.5 / (OBS_VAR * modes)
    info_scale = 1.0 / (OBS_VAR * math.sqrt(modes))
    damp = damp_ref[0:1, :]
    damp_col = damp_cols_ref[:, 0:1]
    wide = damp * damp
    damp_sq = jnp.concatenate([wide, wide], axis=1)

    def shifted(row):
        spread = jnp.broadcast_to(row, (modes, width))
        return pltpu.roll(spread, modes, 1, stride=1, stride_axis=0)[:, :modes]

    most = jnp.zeros((1, width), jnp.float32)
    for step in range(steps):
        near_cos = shifted(sums_ref[step, 0:1, :])
        near_sin = shifted(sums_ref[step, 1:2, :])
        far = jnp.concatenate(
            [shifted(sums_ref[step, 2:3, :]), shifted(sums_ref[step, 3:4, :])], axis=0
        )
        far = exact(far, mirror)
        far_cos, far_sin = far[:modes], far[modes:]
        cosines = turn_ref[step, 0:1, :] * scale
        sines = turn_ref[step, 1:2, :] * scale
        cos_col = turn_cols_ref[step, :, 0:1]
        sin_col = turn_cols_ref[step, :, 1:2]
        up_a, up_b = near_cos + far_cos, far_sin + near_sin
        low_a, low_b = far_sin - near_sin, near_cos - far_cos
        up_left, up_right = up_a * cosines + up_b * sines, up_b * cosines - up_a * sines
        low_left, low_right = low_a * cosines + low_b * sines, low_b * cosines - low_a * sines
        top = jnp.concatenate(
            [cos_col * up_left + sin_col * low_left, cos_col * up_right + sin_col * low_right], axis=1
        )
        bottom = jnp.concatenate(
            [cos_col * low_left - sin_col * up_left, cos_col * low_right - sin_col * up_right], axis=1
        )
        whole = jnp.concatenate([top, bottom], axis=0)
        most = jnp.maximum(most, jnp.sum(jnp.abs(whole), axis=0, keepdims=True))
        edge = 1.0 if step in (0, steps - 1) else 1.0 + damp_sq
        diag[step] = whole + unit * edge
        info_cos, info_sin = sums_ref[step, 4:5, :modes], sums_ref[step, 4:5, modes:]
        turn_cos, turn_sin = turn_ref[step, 0:1, :] * info_scale, turn_ref[step, 1:2, :] * info_scale
        turned = jnp.concatenate(
            [turn_cos * info_cos + turn_sin * info_sin, turn_cos * info_sin - turn_sin * info_cos], axis=1
        )
        info[step] = jnp.broadcast_to(turned, (8, width))
    high = jnp.max(most) * 1.001 + (1.0 + 1.001 * jnp.max(wide))

    def low(power):
        return 0.999 * jnp.min((1.0 - wide) / (1.0 - power))

    def place(position, amount, flipped):
        return jnp.where(flipped, amount - 1 - position, position)

    damp_wide = jnp.concatenate([damp, damp], axis=1)
    damp_tall = jnp.concatenate([damp_col, damp_col], axis=0)
    amount, index, level = steps, own, 0
    power = wide
    diag_at, link_at = 0, 0
    while amount > 1:
        half = amount // 2
        flipped = lax.rem(index, 2) == 1
        links = amount - 1
        out_base = diag_at + amount
        chunk = min(4, half)
        for start in range(0, half, chunk):
            picks = [diag_at + place(2 * k + 1, amount, flipped) for k in range(start, start + chunk)]
            invert(
                [diag.at[pick] for pick in picks],
                [split.at[k] for k in range(chunk)],
                [inverse.at[k] for k in range(start, start + chunk)],
                low(power),
                high,
            )
        for k in range(half):
            kept = diag_at + place(2 * k, amount, flipped)
            diag[out_base + k] = diag[kept]
            info[out_base + k] = info[kept]
        out_links = link_at + (links if level else 0)
        for k in range(half):
            gone = info[diag_at + place(2 * k + 1, amount, flipped)]
            matrix = parts(inverse[k], unit)
            if level == 0:
                moved = damp_tall * matrix[0] * damp_wide
                passed = along(gone, matrix) * damp_wide
                diag[out_base + k] -= moved
                info[out_base + k] += passed
                if k + 1 < half:
                    diag[out_base + k + 1] -= moved
                    info[out_base + k + 1] += passed
                    link[out_links + k] = moved
                    back[out_links + k] = moved
                continue
            here = link_at + place(2 * k, links, flipped)
            forth, revert = link[here], back[here]
            forth, revert = jnp.where(flipped, revert, forth), jnp.where(flipped, forth, revert)
            forth, revert = parts(forth, unit), parts(revert, unit)
            left = parts(near(matrix, revert), unit)
            diag[out_base + k] -= near(forth, left)
            info[out_base + k] += along(gone, left)
            if k + 1 < half:
                after = link_at + place(2 * k + 1, links, flipped)
                next_forth, next_revert = link[after], back[after]
                next_forth, next_revert = (
                    parts(jnp.where(flipped, next_revert, next_forth), unit),
                    parts(jnp.where(flipped, next_forth, next_revert), unit),
                )
                right = parts(near(matrix, next_forth), unit)
                diag[out_base + k + 1] -= near(next_revert, right)
                info[out_base + k + 1] += along(gone, right)
                link[out_links + k] = near(forth, right)
                back[out_links + k] = near(next_revert, left)
        index = place(index, amount, flipped) // 2
        diag_at, link_at = out_base, out_links
        amount, level, power = half, level + 1, power * power

    invert([diag.at[diag_at]], [split.at[0]], [inverse.at[0]], 0.999 * jnp.min(1.0 - wide), high)
    result = inverse[0]
    state = exact(info[diag_at], result)[0:1]
    cosines, sines = turn_ref[own, 0:1, :], turn_ref[own, 1:2, :]
    cos_col, sin_col = turn_cols_ref[own, :, 0:1], turn_cols_ref[own, :, 1:2]
    left, right = result[:, :modes], result[:, modes:]
    left, right = left * cosines - right * sines, left * sines + right * cosines
    result = jnp.concatenate([left, right], axis=1)
    upper, lower = result[:modes], result[modes:]
    result = jnp.concatenate(
        [cos_col * upper - sin_col * lower, sin_col * upper + cos_col * lower], axis=0
    )
    first, second = state[:, :modes], state[:, modes:]
    state = jnp.concatenate([first * cosines - second * sines, first * sines + second * cosines], axis=1)
    block = cov_ref.shape[1]
    out_rows = lax.broadcasted_iota(jnp.int32, (block, width), 0) + block_row * block
    out_cols = lax.broadcasted_iota(jnp.int32, (block, width), 1)
    pick = jnp.where(out_cols == out_rows // 2 + lax.rem(out_rows, 2) * modes, 1.0, 0.0)
    spread = jnp.where(rows == cols // 2 + lax.rem(cols, 2) * modes, 1.0, 0.0)
    cov_ref[0] = exact(exact(pick, result), spread)
    means = lax.dot_general(
        jnp.broadcast_to(state, (8, width)), pick, (((1,), (1,)), ((), ())),
        precision=exact_mode, preferred_element_type=jnp.float32,
    )
    mean_ref[...] = means[0:1]


def local(observations, site_ids, counts, frequencies, decay, proc_var):
    modes = frequencies.shape[0]
    width = 2 * modes
    count = lax.axis_size("tm")
    steps = count * observations.shape[0]
    block = width // lax.axis_size("rows")
    vmem = pl.BlockSpec(memory_space=pltpu.VMEM)
    smem = pl.BlockSpec(memory_space=pltpu.SMEM)
    shared = pl.pallas_call(
        functools.partial(share_kernel, "tm"),
        out_shape=(
            jax.ShapeDtypeStruct((steps, 8, width), jnp.float32),
            jax.ShapeDtypeStruct((steps, 8, modes), jnp.float32),
            jax.ShapeDtypeStruct((steps, modes, 8), jnp.float32),
            jax.ShapeDtypeStruct((8, modes), jnp.float32),
            jax.ShapeDtypeStruct((modes, 8), jnp.float32),
        ),
        in_specs=[smem] + [vmem] * 5,
        out_specs=(vmem,) * 5,
        scratch_shapes=[
            pltpu.VMEM((8, width), jnp.float32),
            pltpu.VMEM((count, 8, width), jnp.float32),
            pltpu.SemaphoreType.DMA((count,)),
            pltpu.SemaphoreType.DMA((count,)),
        ],
        compiler_params=pltpu.CompilerParams(collective_id=0, has_side_effects=True),
        name="share",
    )(counts, site_ids, observations, frequencies[None], decay[None], proc_var[None])
    return pl.pallas_call(
        functools.partial(solve_kernel, "tm", "rows"),
        out_shape=(
            jax.ShapeDtypeStruct((1, block), jnp.float32),
            jax.ShapeDtypeStruct((1, block, width), jnp.float32),
        ),
        in_specs=[vmem] * 5,
        out_specs=(vmem, vmem),
        scratch_shapes=[
            pltpu.VMEM((2 * steps, width, width), jnp.float32),
            pltpu.VMEM((steps, width, width), jnp.float32),
            pltpu.VMEM((steps, width, width), jnp.float32),
            pltpu.VMEM((2 * steps, 8, width), jnp.float32),
            pltpu.VMEM((4, 2, width, width), jnp.bfloat16),
            pltpu.VMEM((max(1, steps // 2), width, width), jnp.float32),
        ],
        name="solve",
    )(*shared)


def solution(mesh):
    return jax.shard_map(
        local,
        mesh=mesh,
        in_specs=(P("tm", None), P("tm", None), P("tm"), P(), P(), P()),
        out_specs=(P("tm", "rows"), P("tm", "rows", None)),
        check_vma=False,
    )
```

```python
import functools
import math

import jax
import jax.numpy as jnp
from jax import lax
from jax.experimental import pallas as pl
from jax.experimental.pallas import tpu as pltpu
from jax.sharding import PartitionSpec as P

GRID = 4096
OBS_VAR = 64
TOLERANCE = 3e-5
INNER_TOLERANCE = 4e-6
FINE = 16

exact_mode = lax.Precision.HIGHEST


def exact(left, right):
    return jnp.dot(left, right, precision=exact_mode, preferred_element_type=jnp.float32)


def coarse(left, right):
    return jnp.dot(
        left.astype(jnp.bfloat16), right.astype(jnp.bfloat16), preferred_element_type=jnp.float32
    )


def halves(value):
    high = value.astype(jnp.bfloat16)
    return high, (value - high.astype(jnp.float32)).astype(jnp.bfloat16)


def product(left, right):
    left_high, left_low = left if isinstance(left, tuple) else halves(left)
    right_high, right_low = right if isinstance(right, tuple) else halves(right)
    dot = functools.partial(jnp.dot, preferred_element_type=jnp.float32)
    return dot(left_high, right_high) + (dot(left_high, right_low) + dot(left_low, right_high))


def spread_by(value, picks):
    high, low = halves(value)
    picks = picks.astype(jnp.bfloat16)
    dot = functools.partial(jnp.dot, preferred_element_type=jnp.float32)
    return dot(high, picks) + dot(low, picks)


def picked_by(picks, value):
    high, low = halves(value)
    picks = picks.astype(jnp.bfloat16)
    dot = functools.partial(jnp.dot, preferred_element_type=jnp.float32)
    return dot(picks, high) + dot(picks, low)


def parts(value, unit):
    marked = value * unit
    off = value - marked
    column = jnp.sum(marked, axis=1, keepdims=True)
    row = jnp.sum(marked, axis=0, keepdims=True)
    return value, off, halves(off), column, row


def near(left, right):
    return product(left[2], right[2]) + left[3] * right[0] + left[1] * right[4]


def along(row, right):
    return product(row, right[2]) + row * right[4]


def circle(angle):
    square = angle * angle
    cosine = 1.0 / 40320.0 - square * (1.0 / 3628800.0)
    cosine = 1.0 - square * (0.5 - square * (1.0 / 24.0 - square * (1.0 / 720.0 - square * cosine)))
    sine = 1.0 / 5040.0 - square * (1.0 / 362880.0)
    sine = angle * (1.0 - square * (1.0 / 6.0 - square * (1.0 / 120.0 - square * sine)))
    return cosine, sine


def quarter_turn(quadrant, cosine, sine):
    odd = (quadrant & 1) == 1
    new_cosine = jnp.where(odd, sine, cosine)
    new_sine = jnp.where(odd, cosine, sine)
    new_cosine = jnp.where(((quadrant + 1) & 2) == 2, -new_cosine, new_cosine)
    new_sine = jnp.where((quadrant & 2) == 2, -new_sine, new_sine)
    return new_cosine, new_sine


def share_kernel(
    tm_axis, counts_ref, site_ref, obs_ref, freq_ref, decay_ref, var_ref,
    sums_ref, turn_ref, cols_ref, damp_ref, damp_cols_ref, mine, held, send_sem, recv_sem,
):
    count = lax.axis_size(tm_axis)
    own = lax.axis_index(tm_axis)
    sites = site_ref.shape[1]
    modes = freq_ref.shape[1]
    steps = sums_ref.shape[0]
    barrier = pltpu.get_barrier_semaphore()
    for offset in range(1, count):
        pl.semaphore_signal(
            barrier, inc=1, device_id={tm_axis: lax.rem(own + offset, count)},
            device_id_type=pl.DeviceIdType.MESH,
        )

    groups = 2 * modes // FINE
    total = 2 * groups + groups // 2 + FINE
    last = total - FINE
    spot = lax.broadcasted_iota(jnp.int32, (total, sites), 0)
    exponent = jnp.where(spot < groups, spot * FINE - modes, 2 * modes + 1 - (spot - groups) * FINE)
    exponent = jnp.where(spot >= 2 * groups, (spot - 2 * groups) * FINE + 1, exponent)
    exponent = jnp.where(spot >= last, spot - last, exponent)
    phase = (exponent * site_ref[...]) & (GRID - 1)
    quadrant = (phase + GRID // 8) >> int(math.log2(GRID // 4))
    angle = (phase - quadrant * (GRID // 4)).astype(jnp.float32) * (2.0 * math.pi / GRID)
    cosines, sines = quarter_turn(quadrant, *circle(angle))
    slots = lax.broadcasted_iota(jnp.int32, (1, sites), 1)
    weights = jnp.where(slots < counts_ref[0], 1.0, 0.0)
    scale = jnp.where(spot[:last] < 2 * groups, weights, weights * obs_ref[...])
    left = jnp.concatenate([cosines[:last] * scale, sines[:last] * scale], axis=0)
    right = jnp.concatenate([cosines[last:], sines[last:]], axis=0)
    left_high, left_low = halves(left)
    right_high, right_low = halves(right)
    beside = functools.partial(
        lax.dot_general,
        dimension_numbers=(((1,), (1,)), ((), ())),
        preferred_element_type=jnp.float32,
    )
    sums = beside(left_high, right_high) + (beside(left_high, right_low) + beside(left_low, right_high))
    wide = lax.broadcasted_iota(jnp.int32, (2 * FINE, 2 * modes), 1)
    tall = lax.broadcasted_iota(jnp.int32, (2 * FINE, 2 * modes), 0)
    by_cos = spread_by(sums, jnp.where(tall == (wide & (FINE - 1)), 1.0, 0.0))
    by_sin = spread_by(sums, jnp.where(tall - FINE == (wide & (FINE - 1)), 1.0, 0.0))
    one, two = groups, 2 * groups
    cc, cs, sc, ss = by_cos[:last], by_sin[:last], by_cos[last:], by_sin[last:]
    lane = lax.broadcasted_iota(jnp.int32, (groups, 2 * modes), 1)
    keep = jnp.where(lane // FINE == lax.broadcasted_iota(jnp.int32, (groups, 2 * modes), 0), 1.0, 0.0)

    def flat(value):
        return jnp.sum(value * keep[: value.shape[0]], axis=0, keepdims=True)

    near_cos = flat((cc - ss)[:one])
    near_sin = flat((sc + cs)[:one])
    far_cos = flat((cc + ss)[one:two])
    far_sin = flat((sc - cs)[one:two])
    info = jnp.concatenate([flat((cc - ss)[two:])[:, :modes], flat((sc + cs)[two:])[:, :modes]], axis=1)
    empty = jnp.zeros((3, 2 * modes), jnp.float32)
    mine[...] = jnp.concatenate([near_cos, near_sin, far_cos, far_sin, info, empty], axis=0)

    pl.semaphore_wait(barrier, count - 1)
    copies = []
    for offset in range(1, count):
        copy = pltpu.make_async_remote_copy(
            src_ref=mine,
            dst_ref=held.at[offset],
            send_sem=send_sem.at[offset],
            recv_sem=recv_sem.at[offset],
            device_id={tm_axis: lax.rem(own + offset, count)},
            device_id_type=pl.DeviceIdType.MESH,
        )
        copy.start()
        copies.append(copy)

    frequency = freq_ref[...]
    turns = jnp.where(jnp.abs(frequency) > 0.25 * math.pi, 1, 0) + jnp.where(
        jnp.abs(frequency) > 0.75 * math.pi, 1, 0
    )
    turns = jnp.where(frequency < 0.0, -turns, turns)
    share = turns.astype(jnp.float32)
    reduced = (frequency - share * 1.5703125) - share * (0.5 * math.pi - 1.5703125)
    cosine, sine = quarter_turn(turns + 4, *circle(reduced))
    damping = jnp.exp(-decay_ref[...])
    now_cos = jnp.sqrt(var_ref[...])
    now_sin = jnp.zeros_like(now_cos)
    for step in range(steps):
        block = jnp.concatenate([now_cos, now_sin, jnp.zeros((modes - 2, modes), jnp.float32)], axis=0)
        turn_ref[step] = block[:8]
        cols_ref[step] = block.T[:, :8]
        now_cos, now_sin = now_cos * cosine - now_sin * sine, now_cos * sine + now_sin * cosine
    spread = jnp.broadcast_to(damping, (modes, modes))
    damp_ref[...] = spread[:8]
    damp_cols_ref[...] = spread.T[:, :8]

    sums_ref[own] = mine[...]
    for offset in range(1, count):
        copies[offset - 1].wait()
        sums_ref[lax.rem(own + count - offset, count)] = held[offset]


def invert(sources, targets, low, high, tolerance):
    width = sources[0].shape[-1]
    rows = lax.broadcasted_iota(jnp.int32, (width, width), 0)
    unit = jnp.where(rows == lax.broadcasted_iota(jnp.int32, (width, width), 1), 1.0, 0.0)
    center = (high + low) / (high - low)
    slope = 2.0 / (high - low)
    top = 2.0 * center * center - 1.0
    scaled = []
    bound = 0.0
    for source in sources:
        matrix = source[...]
        marked = matrix * unit
        tall = lax.rsqrt(jnp.sum(marked, axis=1, keepdims=True))
        wide = lax.rsqrt(jnp.sum(marked, axis=0, keepdims=True))
        off = (matrix - marked) * tall * wide
        parted = halves(off)
        square = product(parted, parted)
        bound = jnp.maximum(bound, jnp.max(jnp.sum(jnp.abs(square), axis=0, keepdims=True)))
        scaled.append((tall, wide, off, parted[0], square))
    good = bound < 0.81
    bound = jnp.minimum(bound * 1.001, 0.81)
    start = bound / (2.0 - bound)
    gain = 4.0 / ((2.0 - start * start) * (2.0 - bound))
    for source, target, (tall, wide, off, high_off, square) in zip(sources, targets, scaled):
        residue = (2.0 * square - bound * unit) * (1.0 / (2.0 - bound))
        moved = jnp.dot(high_off, residue.astype(jnp.bfloat16), preferred_element_type=jnp.float32)
        taken = gain * (unit - off + residue - moved) * tall * wide
        other = (4.0 * center * slope / top) * unit - (2.0 * slope * slope / top) * source[...]
        target[...] = jnp.where(good, taken, other)

    def body(radius):
        factor = 2.0 / (2.0 - radius * radius)
        residues = []
        for source, target in zip(sources, targets):
            marked = target[...] * unit
            row = jnp.sum(marked, axis=0, keepdims=True)
            matrix = source[...]
            base = matrix * unit
            off = matrix - base
            column = jnp.sum(base, axis=1, keepdims=True)
            residues.append(
                (unit - column * target[...]) - off * row - product(halves(off), target[...] - marked)
            )
        for target, residue in zip(targets, residues):
            target[...] = factor * (target[...] + coarse(target[...], residue))
        return radius * radius / (2.0 - radius * radius)

    first = jnp.where(good, start * start / (2.0 - start * start), 1.0 / top)
    lax.while_loop(lambda radius: radius > tolerance, body, first)


def solve_kernel(
    tm_axis, rows_axis, sums_ref, turn_ref, turn_cols_ref, damp_ref, damp_cols_ref,
    mean_ref, cov_ref, diag, link, back, info, inverse,
):
    steps = sums_ref.shape[0]
    width = sums_ref.shape[2]
    modes = width // 2
    own = lax.axis_index(tm_axis)
    block_row = lax.axis_index(rows_axis)
    rows = lax.broadcasted_iota(jnp.int32, (width, width), 0)
    cols = lax.broadcasted_iota(jnp.int32, (width, width), 1)
    unit = jnp.where(rows == cols, 1.0, 0.0)
    small_rows = lax.broadcasted_iota(jnp.int32, (modes, modes), 0)
    small_cols = lax.broadcasted_iota(jnp.int32, (modes, modes), 1)
    mirror = jnp.where(small_rows + small_cols == modes - 1, 1.0, 0.0)
    scale = 0.5 / (OBS_VAR * modes)
    info_scale = 1.0 / (OBS_VAR * math.sqrt(modes))
    damp = damp_ref[0:1, :]
    damp_col = damp_cols_ref[:, 0:1]
    wide = damp * damp
    damp_sq = jnp.concatenate([wide, wide], axis=1)

    def shifted(row):
        spread = jnp.broadcast_to(row, (modes, width))
        return pltpu.roll(spread, modes, 1, stride=1, stride_axis=0)[:, :modes]

    most = jnp.zeros((1, width), jnp.float32)
    far_all = spread_by(
        jnp.concatenate(
            [shifted(sums_ref[step, row : row + 1, :]) for step in range(steps) for row in (2, 3)], axis=0
        ),
        mirror,
    )
    for step in range(steps):
        near_cos = shifted(sums_ref[step, 0:1, :])
        near_sin = shifted(sums_ref[step, 1:2, :])
        far_cos = far_all[2 * step * modes : (2 * step + 1) * modes]
        far_sin = far_all[(2 * step + 1) * modes : (2 * step + 2) * modes]
        cosines = turn_ref[step, 0:1, :] * scale
        sines = turn_ref[step, 1:2, :] * scale
        cos_col = turn_cols_ref[step, :, 0:1]
        sin_col = turn_cols_ref[step, :, 1:2]
        up_a, up_b = near_cos + far_cos, far_sin + near_sin
        low_a, low_b = far_sin - near_sin, near_cos - far_cos
        up_left, up_right = up_a * cosines + up_b * sines, up_b * cosines - up_a * sines
        low_left, low_right = low_a * cosines + low_b * sines, low_b * cosines - low_a * sines
        top = jnp.concatenate(
            [cos_col * up_left + sin_col * low_left, cos_col * up_right + sin_col * low_right], axis=1
        )
        bottom = jnp.concatenate(
            [cos_col * low_left - sin_col * up_left, cos_col * low_right - sin_col * up_right], axis=1
        )
        whole = jnp.concatenate([top, bottom], axis=0)
        most = jnp.maximum(most, jnp.sum(jnp.abs(whole), axis=0, keepdims=True))
        edge = 1.0 if step in (0, steps - 1) else 1.0 + damp_sq
        diag[step] = whole + unit * edge
        info_cos, info_sin = sums_ref[step, 4:5, :modes], sums_ref[step, 4:5, modes:]
        turn_cos, turn_sin = turn_ref[step, 0:1, :] * info_scale, turn_ref[step, 1:2, :] * info_scale
        turned = jnp.concatenate(
            [turn_cos * info_cos + turn_sin * info_sin, turn_cos * info_sin - turn_sin * info_cos], axis=1
        )
        info[step] = jnp.broadcast_to(turned, (8, width))
    high = jnp.max(most) * 1.001 + (1.0 + 1.001 * jnp.max(wide))

    def low(power):
        return 0.999 * jnp.min((1.0 - wide) / (1.0 - power))

    def place(position, amount, flipped):
        return jnp.where(flipped, amount - 1 - position, position)

    damp_wide = jnp.concatenate([damp, damp], axis=1)
    damp_tall = jnp.concatenate([damp_col, damp_col], axis=0)
    amount, index, level = steps, own, 0
    power = wide
    diag_at, link_at = 0, 0
    while amount > 1:
        half = amount // 2
        flipped = lax.rem(index, 2) == 1
        links = amount - 1
        out_base = diag_at + amount
        chunk = min(4, half)
        for start in range(0, half, chunk):
            picks = [diag_at + place(2 * k + 1, amount, flipped) for k in range(start, start + chunk)]
            invert(
                [diag.at[pick] for pick in picks],
                [inverse.at[k] for k in range(start, start + chunk)],
                low(power),
                high,
                INNER_TOLERANCE,
            )
        for k in range(half):
            kept = diag_at + place(2 * k, amount, flipped)
            diag[out_base + k] = diag[kept]
            info[out_base + k] = info[kept]
        out_links = link_at + (links if level else 0)
        for k in range(half):
            gone = info[diag_at + place(2 * k + 1, amount, flipped)]
            matrix = parts(inverse[k], unit)
            if level == 0:
                moved = damp_tall * matrix[0] * damp_wide
                passed = along(gone, matrix) * damp_wide
                diag[out_base + k] -= moved
                info[out_base + k] += passed
                if k + 1 < half:
                    diag[out_base + k + 1] -= moved
                    info[out_base + k + 1] += passed
                    link[out_links + k] = moved
                continue
            here = link_at + place(2 * k, links, flipped)
            if level == 1:
                forth = revert = parts(link[here], unit)
            else:
                forth, revert = link[here], back[here]
                forth, revert = (
                    parts(jnp.where(flipped, revert, forth), unit),
                    parts(jnp.where(flipped, forth, revert), unit),
                )
            left = parts(near(matrix, revert), unit)
            diag[out_base + k] -= near(forth, left)
            info[out_base + k] += along(gone, left)
            if k + 1 < half:
                after = link_at + place(2 * k + 1, links, flipped)
                if level == 1:
                    next_forth = next_revert = parts(link[after], unit)
                else:
                    next_forth, next_revert = link[after], back[after]
                    next_forth, next_revert = (
                        parts(jnp.where(flipped, next_revert, next_forth), unit),
                        parts(jnp.where(flipped, next_forth, next_revert), unit),
                    )
                right = parts(near(matrix, next_forth), unit)
                diag[out_base + k + 1] -= near(next_revert, right)
                info[out_base + k + 1] += along(gone, right)
                link[out_links + k] = near(forth, right)
                back[out_links + k] = near(next_revert, left)
        index = place(index, amount, flipped) // 2
        diag_at, link_at = out_base, out_links
        amount, level, power = half, level + 1, power * power

    invert([diag.at[diag_at]], [inverse.at[0]], 0.999 * jnp.min(1.0 - wide), high, TOLERANCE)
    result = inverse[0]
    state = along(info[diag_at], parts(result, unit))[0:1]
    cosines, sines = turn_ref[own, 0:1, :], turn_ref[own, 1:2, :]
    cos_col, sin_col = turn_cols_ref[own, :, 0:1], turn_cols_ref[own, :, 1:2]
    left, right = result[:, :modes], result[:, modes:]
    left, right = left * cosines - right * sines, left * sines + right * cosines
    result = jnp.concatenate([left, right], axis=1)
    upper, lower = result[:modes], result[modes:]
    result = jnp.concatenate(
        [cos_col * upper - sin_col * lower, sin_col * upper + cos_col * lower], axis=0
    )
    first, second = state[:, :modes], state[:, modes:]
    state = jnp.concatenate([first * cosines - second * sines, first * sines + second * cosines], axis=1)
    block = cov_ref.shape[1]
    out_rows = lax.broadcasted_iota(jnp.int32, (block, width), 0) + block_row * block
    out_cols = lax.broadcasted_iota(jnp.int32, (block, width), 1)
    pick = jnp.where(out_cols == out_rows // 2 + lax.rem(out_rows, 2) * modes, 1.0, 0.0)
    spread = jnp.where(rows == cols // 2 + lax.rem(cols, 2) * modes, 1.0, 0.0)
    cov_ref[0] = spread_by(picked_by(pick, result), spread)
    means = lax.dot_general(
        jnp.broadcast_to(state, (8, width)), pick, (((1,), (1,)), ((), ())),
        precision=exact_mode, preferred_element_type=jnp.float32,
    )
    mean_ref[...] = means[0:1]


def local(observations, site_ids, counts, frequencies, decay, proc_var):
    modes = frequencies.shape[0]
    width = 2 * modes
    count = lax.axis_size("tm")
    steps = count * observations.shape[0]
    block = width // lax.axis_size("rows")
    vmem = pl.BlockSpec(memory_space=pltpu.VMEM)
    smem = pl.BlockSpec(memory_space=pltpu.SMEM)
    shared = pl.pallas_call(
        functools.partial(share_kernel, "tm"),
        out_shape=(
            jax.ShapeDtypeStruct((steps, 8, width), jnp.float32),
            jax.ShapeDtypeStruct((steps, 8, modes), jnp.float32),
            jax.ShapeDtypeStruct((steps, modes, 8), jnp.float32),
            jax.ShapeDtypeStruct((8, modes), jnp.float32),
            jax.ShapeDtypeStruct((modes, 8), jnp.float32),
        ),
        in_specs=[smem] + [vmem] * 5,
        out_specs=(vmem,) * 5,
        scratch_shapes=[
            pltpu.VMEM((8, width), jnp.float32),
            pltpu.VMEM((count, 8, width), jnp.float32),
            pltpu.SemaphoreType.DMA((count,)),
            pltpu.SemaphoreType.DMA((count,)),
        ],
        compiler_params=pltpu.CompilerParams(collective_id=0, has_side_effects=True),
        name="share",
    )(counts, site_ids, observations, frequencies[None], decay[None], proc_var[None])
    return pl.pallas_call(
        functools.partial(solve_kernel, "tm", "rows"),
        out_shape=(
            jax.ShapeDtypeStruct((1, block), jnp.float32),
            jax.ShapeDtypeStruct((1, block, width), jnp.float32),
        ),
        in_specs=[vmem] * 5,
        out_specs=(vmem, vmem),
        scratch_shapes=[
            pltpu.VMEM((2 * steps, width, width), jnp.float32),
            pltpu.VMEM((steps, width, width), jnp.float32),
            pltpu.VMEM((steps, width, width), jnp.float32),
            pltpu.VMEM((2 * steps, 8, width), jnp.float32),
            pltpu.VMEM((max(1, steps // 2), width, width), jnp.float32),
        ],
        name="solve",
    )(*shared)


def solution(mesh):
    return jax.shard_map(
        local,
        mesh=mesh,
        in_specs=(P("tm", None), P("tm", None), P("tm"), P(), P(), P()),
        out_specs=(P("tm", "rows"), P("tm", "rows", None)),
        check_vma=False,
    )
```
